32 devices in a mesh: row: 8 (over y, x, core), col: 4 (over z).
Axes of the slice: x: 2, y: 2, z: 4, core: 2. Of those that a mesh axis runs over, the one named last changes fastest.
Arguments:
- right_sides: float32 [64, 32768], P(None, ('row', 'col'))
- diag_tiles: float32 [32, 1024, 1024], P(('row', 'col')), as said below
- low_rank: float32 [32, 4, 8, 2, 12, 1024], P('row', 'col'), as said below
- tile_ranks: int32 [32, 4, 8], P('row', 'col'), may hold values from 1 to 12, as said below
- inv_factor: float32 [256, 8, 128, 128], P(('row', 'col')), as said below
- sub_sizes: int32 [64], replicated, may hold values from 1 to 8, 256 in all
Outputs:
- solution: float32 [64, 32768], P(None, ('row', 'col'))
- residual: float32 [64, 32768], P(None, ('row', 'col'))
The draws below stay inside these ranges and needn't reach their ends.
Inputs may be any that keep to these rules, and one draw needn't show every extreme that they name: `low_rank`: tile (j, i) holds the two factors of tile (i, j) in swapped order, and a diagonal tile's two factors are equal, so S is symmetric. `tile_ranks`: the rank of tile (i, j) equals that of tile (j, i); diagonal tiles have rank 12. `diag_tiles`: each tile is symmetric positive definite. `inv_factor`: the block at distance 0 of every span is lower triangular with a positive diagonal. `sub_sizes`: the sizes sum to 256.
All inputs are finite; a program needn't handle non-finite values.
Results may differ from the reference program's by a relative error of at most 0.0003.
Values sent between devices are 32-bit elements; how exact they have to be, the bound alone decides.
A program may use at most 128 MiB of HBM per device.

```python
import math
import jax
import jax.numpy as jnp
import numpy as np
from jax import lax

RHS = 64
TILE = 1024
RANK = 12
SPAN = 128
MAXC = 8
STRIDE = 4
GROUPS = 8
NT = 32
ORDER = 32768
NCHUNK = 256
SUBS = 64


def draw_right_sides(key, part):
    fraction = lax.iota(jnp.float32, ORDER) / ORDER
    rising = 1.0 + 2.0 * fraction
    values = jax.random.normal(key, (RHS, ORDER), jnp.float32) * rising
    return values


def draw_diag_tiles(key, part):
    noise_key, diag_key = jax.random.split(key)
    noises = jax.random.normal(noise_key, (NT, TILE, TILE), jnp.float32)
    symmetric = (noises + jnp.swapaxes(noises, 1, 2)) * (0.42 / math.sqrt(TILE))
    diagonal = jnp.exp(jax.random.uniform(diag_key, (NT, TILE, 1), jnp.float32, math.log(2.2), math.log(4.4)))
    identity = (lax.iota(jnp.int32, TILE)[:, None] == lax.iota(jnp.int32, TILE)[None, :]).astype(jnp.float32)
    return symmetric + diagonal * identity[None]


def draw_low_rank(key, part):
    spread_scale = 0.45 * (ORDER * RANK) ** (-0.25)
    slot_ids = lax.iota(jnp.int32, STRIDE)
    group_ids = lax.iota(jnp.int32, GROUPS)

    def one_tile(row_index, col_slot, group):
        col_index = group * STRIDE + col_slot
        pair_index = jnp.minimum(row_index, col_index) * NT + jnp.maximum(row_index, col_index)
        tile_key = jax.random.fold_in(key, pair_index)
        noises = jax.random.normal(tile_key, (2, RANK, TILE), jnp.float32)
        left_part = jnp.where(row_index < col_index, noises[1], noises[0])
        right_part = jnp.where(row_index > col_index, noises[1], noises[0])
        return jnp.stack([left_part, right_part]) * spread_scale

    def tile_row(row_index):

        def by_slot(col_slot):

            def by_group(group):
                return one_tile(row_index, col_slot, group)
            return jax.vmap(by_group)(group_ids)
        return jax.vmap(by_slot)(slot_ids)
    return lax.map(tile_row, lax.iota(jnp.int32, NT))


def draw_tile_ranks(key, part):
    drawn = jax.random.randint(key, (NT, NT), 1, RANK + 1)
    row_ids = lax.iota(jnp.int32, NT)[:, None]
    col_ids = lax.iota(jnp.int32, NT)[None, :]
    mirrored = jnp.where(row_ids > col_ids, drawn, drawn.T)
    mirrored = jnp.where(row_ids == col_ids, RANK, mirrored)
    return mirrored.reshape(NT, GROUPS, STRIDE).transpose(0, 2, 1)


def draw_inv_factor(key, part):
    noise_key, diag_key = jax.random.split(key)
    shape_all = (NCHUNK, MAXC, SPAN, SPAN)
    noises = jax.random.normal(noise_key, shape_all, jnp.float32)
    out_ids = lax.iota(jnp.int32, SPAN)[:, None]
    in_ids = lax.iota(jnp.int32, SPAN)[None, :]
    strict = (in_ids < out_ids).astype(jnp.float32)
    identity = (in_ids == out_ids).astype(jnp.float32)
    pivots = jnp.exp(jax.random.uniform(diag_key, (NCHUNK, 1, SPAN, 1), jnp.float32, 0.0, math.log(2.0)))
    slot_zero = noises * strict * (0.4 / math.sqrt(SPAN)) + pivots * identity
    others = noises * (0.4 / math.sqrt(SPAN * MAXC))
    first_slot = (lax.iota(jnp.int32, MAXC) == 0)[None, :, None, None]
    return jnp.where(first_slot, slot_zero, others)


def length_profile(count, total, bound, lean):
    portions = [(1 << 20) // math.isqrt(grade ** lean) + 1 for grade in range(2, count + 1)]
    surplus, given = total - bound - (count - 1), [1] * (count - 1)
    while surplus > 0:
        free = [i for i in range(count - 1) if given[i] < bound]
        mass, remaining = sum([portions[i] for i in free]), surplus
        for i in free:
            addition = min(bound - given[i], max(1, remaining * portions[i] // mass), surplus)
            given[i] = given[i] + addition
            surplus = surplus - addition
    return np.array([bound] + given)


def ragged(key, number_of, total, most, lean):
    if number_of == 2:
        one = jax.random.randint(key, (), max(1, total - most), min(most, total - 1) + 1)
        return jnp.stack([one, total - one])
    lengths = jnp.asarray(length_profile(number_of, total, most, lean), jnp.int32)
    pairs = (number_of - 1) // 2
    giver, receiver = lengths[1:1 + 2 * pairs:2], lengths[2:2 + 2 * pairs:2]
    slack = jnp.minimum(giver - 1, most - receiver)
    moved = jax.random.randint(jax.random.fold_in(key, 1), (pairs,), 0, 1 << 20) % (slack + 1)
    lengths = lengths.at[1:1 + 2 * pairs:2].set(giver - moved).at[2:2 + 2 * pairs:2].set(receiver + moved)
    return lengths[jax.random.permutation(jax.random.fold_in(key, 2), number_of)]


def setup_inputs(seed: int = 0) -> dict:
    key_list = jax.random.split(jax.random.key(seed), 7)
    return {
        "right_sides": draw_right_sides(jax.random.fold_in(key_list[6], 71), 0),
        "diag_tiles": draw_diag_tiles(jax.random.fold_in(key_list[6], 71), 0),
        "low_rank": draw_low_rank(jax.random.fold_in(key_list[6], 71), 0),
        "tile_ranks": draw_tile_ranks(jax.random.fold_in(key_list[6], 71), 0),
        "inv_factor": draw_inv_factor(jax.random.fold_in(key_list[6], 71), 0),
        "sub_sizes": ragged(key_list[5], SUBS, NCHUNK, MAXC, 2).astype(jnp.int32),
    }


finest = lax.Precision.HIGHEST

def span_weights(span_ids, sub_sizes):
    ending = jnp.cumsum(sub_sizes).astype(jnp.int32)
    opening = (ending - sub_sizes).astype(jnp.int32)
    inside = (span_ids[:, None] >= opening[None, :]) & (span_ids[:, None] < ending[None, :])
    position = span_ids - jnp.sum(jnp.where(inside, opening[None, :], 0), axis=1).astype(jnp.int32)
    return (lax.iota(jnp.int32, MAXC)[None, :] <= position[:, None]).astype(jnp.float32)

def precondition(vector, inv_factor, weights):
    blocks = vector.reshape(RHS, NCHUNK, SPAN)
    padded = jnp.pad(blocks, ((0, 0), (MAXC, 0), (0, 0)))
    windows = jnp.stack([padded[:, MAXC - behind:MAXC - behind + NCHUNK] for behind in range(MAXC)], axis=2)
    windows = windows * weights[None, :, :, None]
    forward = jnp.einsum('ltji,klti->klj', inv_factor, windows, precision=finest)
    spread = jnp.einsum('ltji,klj->klti', inv_factor, forward, precision=finest) * weights[None, :, :, None]
    result = jnp.zeros_like(blocks)
    for behind in range(MAXC):
        result = result + jnp.pad(spread[:, behind:, behind], ((0, 0), (0, behind), (0, 0)))
    return result.reshape(RHS, ORDER)

def operate(vector, diag_tiles, low_rank, tile_ranks):
    tiles_in = vector.reshape(RHS, NT, TILE)
    local_part = jnp.einsum('kit,its->kis', tiles_in, diag_tiles, precision=finest)

    def tile_row(row_item):
        factors, row_ranks = row_item
        ordered = jnp.swapaxes(factors, 0, 1).reshape(NT, 2, RANK, TILE)
        ordered_ranks = jnp.swapaxes(row_ranks, 0, 1).reshape(NT)
        weight = (lax.iota(jnp.int32, RANK)[None, :] < ordered_ranks[:, None]).astype(jnp.float32)
        coeffs = jnp.einsum('jqt,kjt->jqk', ordered[:, 1], tiles_in, precision=finest) * weight[:, :, None]
        return jnp.einsum('jqt,jqk->kt', ordered[:, 0], coeffs, precision=finest)
    far_part = lax.map(tile_row, (low_rank, tile_ranks))
    return (local_part + jnp.swapaxes(far_part, 0, 1)).reshape(RHS, ORDER)

def solve_spd(matrix, target):
    factor = jnp.linalg.cholesky(matrix)
    return jax.scipy.linalg.cho_solve((factor, True), target)

def gram_of(first_block, second_block):
    return jnp.dot(first_block, second_block.T, precision=finest)

def apply_coeffs(coeffs, block_rows):
    return jnp.dot(coeffs.T, block_rows, precision=finest)

def reference(right_sides, diag_tiles, low_rank, tile_ranks, inv_factor, sub_sizes):
    weights = span_weights(lax.iota(jnp.int32, NCHUNK), sub_sizes)
    residual = right_sides
    search = precondition(residual, inv_factor, weights)
    rho_now = gram_of(search, residual)
    images = operate(search, diag_tiles, low_rank, tile_ranks)
    step_size = solve_spd(gram_of(search, images), rho_now)
    solution = apply_coeffs(step_size, search)
    residual = residual - apply_coeffs(step_size, images)
    precond = precondition(residual, inv_factor, weights)
    rho_next = gram_of(precond, residual)
    beta_mix = solve_spd(rho_now, rho_next)
    search = precond + apply_coeffs(beta_mix, search)
    images = operate(search, diag_tiles, low_rank, tile_ranks)
    step_size = solve_spd(gram_of(search, images), rho_next)
    solution = solution + apply_coeffs(step_size, search)
    residual = residual - apply_coeffs(step_size, images)
    return (solution, residual)
```

```python
import functools

import jax
import jax.numpy as jnp
from jax import lax
from jax.experimental import pallas as pl
from jax.experimental.pallas import tpu as pltpu
from jax.sharding import PartitionSpec as P

MESH = pl.DeviceIdType.MESH
F32 = jnp.float32
BF16 = jnp.bfloat16
LOW = 8


def split(x):
    high = x.astype(BF16)
    return high, (x - high.astype(F32)).astype(BF16)


def stacked(x):
    high, low = split(x)
    return jnp.concatenate([high, low], axis=0)


def dot_nt(a, b):
    return lax.dot_general(a, b, (((1,), (1,)), ((), ())), preferred_element_type=F32)


def dot_nn(a, b):
    return lax.dot_general(a, b, (((1,), (0,)), ((), ())), preferred_element_type=F32)


def product3(dot, both, high, low):
    rows = both.shape[0] // 2
    first = dot(both, high)
    return first[:rows] + (first[rows:] + dot(both[:rows], low))


def gram(a, b):
    return lax.dot_general(
        a, b, (((1,), (1,)), ((), ())), precision=lax.Precision.HIGHEST, preferred_element_type=F32
    )


def mixed(coeffs, rows):
    return jnp.dot(coeffs, rows, precision=lax.Precision.HIGHEST, preferred_element_type=F32)


def eliminate(work):
    count = work.shape[0]
    row_ids = lax.broadcasted_iota(jnp.int32, work.shape, 0)
    for k in range(count):
        row = work[k : k + 1, :] / work[k : k + 1, k : k + 1]
        work = jnp.where(row_ids == k, row, work - work[:, k : k + 1] * row)
    return work.T[count:, :]


def kernel(
    rows, cols,
    x_ref, diag_ref, ua_ref, ub_ref, inv_ref, sizes_ref,
    sol_ref, res_ref,
    inv_f32, inv_hi, inv_lo, diag_f32, diag_hi, diag_lo, ua_f32, ub_f32, u_hi, u_lo,
    joined, halo_in, back_out, back_in, spread, vec_z, vec_q, coef_out, coef_in, sum_row, sum_col,
    inv_sem, diag_sem, own_sem, u_send, u_recv, halo_send, halo_recv, back_send, back_recv,
    coef_send, coef_recv, row_send, row_recv, col_send, col_recv,
):
    my_row, my_col = lax.axis_index("row"), lax.axis_index("col")
    total = rows * cols
    me = my_row * cols + my_col
    rhs, tile = x_ref.shape
    spans, reach, span, _ = inv_ref.shape
    halo = (reach - 1) * span
    wide = reach * span

    def coords(device):
        return (device // cols, device % cols)

    following = coords((me + 1) % total)
    previous = coords((me + total - 1) % total)

    barrier = pltpu.get_barrier_semaphore()

    def greet(step, carry):
        pl.semaphore_signal(
            barrier, inc=1, device_id=coords((me + step) % total), device_id_type=MESH
        )
        return carry

    lax.fori_loop(1, total, greet, 0)

    inv_copies = []
    for a in range(spans):
        for t in range(reach):
            copy = pltpu.make_async_copy(
                inv_ref.at[a, t],
                inv_f32.at[a, :, (reach - 1 - t) * span : (reach - t) * span],
                inv_sem.at[a],
            )
            copy.start()
    diag_copy = pltpu.make_async_copy(diag_ref.at[0], diag_f32, diag_sem)
    diag_copy.start()
    ua_rows, ub_rows = ua_ref.shape[1], ub_ref.shape[1]

    def at_rows(ref, index, size):
        return ref.at[pl.ds(pl.multiple_of(index * size, size), size), :]

    own_a = pltpu.make_async_copy(ua_ref.at[my_row], at_rows(ua_f32, my_row, ua_rows), own_sem.at[0])
    own_b = pltpu.make_async_copy(ub_ref.at[my_row], at_rows(ub_f32, my_row, ub_rows), own_sem.at[1])
    own_a.start()
    own_b.start()
    pl.semaphore_wait(barrier, total - 1)

    def remote(src, dst, send, recv, device):
        return pltpu.make_async_remote_copy(
            src_ref=src, dst_ref=dst, send_sem=send, recv_sem=recv, device_id=device,
            device_id_type=MESH,
        )

    def halo_copy(src, call):
        return remote(
            src.at[:, tile - halo : tile], halo_in.at[call], halo_send.at[call],
            halo_recv.at[call], following,
        )

    first_halo = halo_copy(x_ref, 0)
    first_halo.start()

    def send_factors(step, carry):
        peer = (my_row + step) % rows
        remote(ua_ref.at[peer], at_rows(ua_f32, my_row, ua_rows), u_send.at[0, step],
               u_recv.at[0, step], (peer, my_col)).start()
        remote(ub_ref.at[peer], at_rows(ub_f32, my_row, ub_rows), u_send.at[1, step],
               u_recv.at[1, step], (peer, my_col)).start()
        return carry

    lax.fori_loop(1, rows, send_factors, 0)

    subs = sizes_ref.shape[1]
    sizes = jnp.broadcast_to(sizes_ref[...].astype(F32), (subs, subs))
    down = lax.broadcasted_iota(jnp.int32, (subs, subs), 0)
    across = lax.broadcasted_iota(jnp.int32, (subs, subs), 1)
    opening = jnp.sum(jnp.where(across < down, sizes, 0.0), axis=1, keepdims=True)
    behind = (reach - 1) - lax.broadcasted_iota(jnp.int32, (1, wide), 1) // span
    behind = behind.astype(F32)

    vec = x_ref[...]
    joined[:, halo:] = stacked(vec)

    for a in range(spans):
        for t in range(reach):
            pltpu.make_async_copy(
                inv_ref.at[a, t], inv_f32.at[a, :, t * span : (t + 1) * span], inv_sem.at[a]
            ).wait()
        number = (me * spans + a).astype(F32)
        start = jnp.max(jnp.where(opening <= number, opening, 0.0), axis=0, keepdims=True)
        mask = jnp.where(behind <= number - start, 1.0, 0.0)
        high, low = split(inv_f32[a] * mask)
        inv_hi[a] = high
        inv_lo[a] = low

    def forward_own():
        parts = []
        for a in range(spans):
            skip = max(0, halo - a * span)
            parts.append(product3(
                dot_nt, joined[:, a * span + skip : a * span + wide],
                inv_hi[a, :, skip:], inv_lo[a, :, skip:],
            ))
        return parts

    def forward_halo(parts, call):
        joined[:, :halo] = stacked(halo_in[call])
        out = []
        for a in range(spans):
            skip = max(0, halo - a * span)
            part = parts[a]
            if skip:
                part = part + product3(
                    dot_nt, joined[:, a * span : halo], inv_hi[a, :, :skip], inv_lo[a, :, :skip]
                )
            out.append(stacked(part))
        return out

    def backward_halo(forward, call):
        spread[:, :halo] = jnp.zeros((rhs, halo), F32)
        for a in range(spans):
            skip = max(0, halo - a * span)
            if skip:
                spread[:, a * span : halo] += product3(
                    dot_nn, forward[a], inv_hi[a, :, :skip], inv_lo[a, :, :skip]
                )
        back_out[call] = spread[:, :halo]
        copy = remote(back_out.at[call], back_in.at[call], back_send.at[call],
                      back_recv.at[call], previous)
        copy.start()
        return copy

    def backward_own(forward):
        spread[:, halo:] = jnp.zeros((rhs, tile), F32)
        for a in range(spans):
            skip = max(0, halo - a * span)
            spread[:, a * span + skip : a * span + wide] += product3(
                dot_nn, forward[a], inv_hi[a, :, skip:], inv_lo[a, :, skip:]
            )

    def returned(call):
        spread[:, halo + tile - halo :] += back_in[call]
        return spread[:, halo:]

    def send_coeffs(both, call):
        wide_part = dot_nt(u_hi[...], both)
        coeffs = wide_part[:, :rhs] + (wide_part[:, rhs:] + dot_nt(u_lo[...], both[:rhs]))
        half = coeffs.shape[0] // 2
        coef_out[call, :, :rhs] = coeffs[:half]
        coef_out[call, :, rhs:] = coeffs[half:]

        def send(step, carry):
            peer = (me + step) % total
            remote(at_rows(coef_out.at[call], peer, LOW), at_rows(coef_in.at[call], me, LOW),
                   coef_send.at[call], coef_recv.at[call], coords(peer)).start()
            return carry

        lax.fori_loop(1, total, send, 0)
        pltpu.make_async_copy(
            at_rows(coef_out.at[call], me, LOW), at_rows(coef_in.at[call], me, LOW), own_sem.at[2 + call]
        ).start()

    def wait_coeffs(call):
        piece = coef_out.at[call, : (total - 1) * LOW, :]
        pltpu.make_async_copy(piece, piece, coef_recv.at[call]).wait()
        pltpu.make_async_copy(
            at_rows(coef_out.at[call], me, LOW), at_rows(coef_in.at[call], me, LOW), own_sem.at[2 + call]
        ).wait()
        turned = coef_in[call].T
        return stacked(jnp.concatenate([turned[:rhs], turned[rhs:]], axis=1))

    def far_part(call):
        return product3(dot_nn, wait_coeffs(call), u_hi[...], u_lo[...])

    def start_sum(value, call):
        sum_row[call, my_row] = value
        for step in range(1, rows):
            remote(sum_row.at[call, my_row], sum_row.at[call, my_row], row_send.at[call],
                   row_recv.at[call], ((my_row + step) % rows, my_col)).start()

    def middle_sum(call):
        piece = sum_row.at[call, : rows - 1]
        pltpu.make_async_copy(piece, piece, row_recv.at[call]).wait()
        sum_col[call, my_col] = jnp.sum(sum_row[call], axis=0)
        for step in range(1, cols):
            remote(sum_col.at[call, my_col], sum_col.at[call, my_col], col_send.at[call],
                   col_recv.at[call], (my_row, (my_col + step) % cols)).start()

    def end_sum(call):
        piece = sum_col.at[call, : cols - 1]
        pltpu.make_async_copy(piece, piece, col_recv.at[call]).wait()
        return jnp.sum(sum_col[call], axis=0)

    parts = forward_own()
    first_halo.wait_recv()
    forward = forward_halo(parts, 0)
    first_back = backward_halo(forward, 0)
    backward_own(forward)
    diag_copy.wait()

    def split_diag(step, carry):
        where = pl.ds(pl.multiple_of(step * span, span), span)
        high, low = split(diag_f32[where, :])
        diag_hi[where, :] = high
        diag_lo[where, :] = low
        return carry

    lax.fori_loop(0, tile // span, split_diag, 0)
    own_a.wait()
    own_b.wait()

    def wait_factors(step, carry):
        peer = (my_row + step) % rows
        remote(ua_ref.at[peer], at_rows(ua_f32, my_row, ua_rows), u_send.at[0, step],
               u_recv.at[0, step], (peer, my_col)).wait()
        remote(ub_ref.at[peer], at_rows(ub_f32, my_row, ub_rows), u_send.at[1, step],
               u_recv.at[1, step], (peer, my_col)).wait()
        return carry

    lax.fori_loop(1, rows, wait_factors, 0)
    tail = ub_f32.shape[0] // total
    upper = lax.broadcasted_iota(jnp.int32, (LOW, tile), 0) < tail

    def split_factors(step, carry):
        where = pl.ds(pl.multiple_of(step * 2 * LOW, 2 * LOW), 2 * LOW)
        high, low = split(ua_f32[where, :])
        u_hi[where, :] = high
        u_lo[where, :] = low
        pair = ub_f32[pl.ds(pl.multiple_of(step * LOW, LOW), LOW), :]
        other = jnp.concatenate([pair[tail:], pair[:tail]], axis=0)
        both = jnp.concatenate([jnp.where(upper, pair, 0.0), jnp.where(upper, other, 0.0)], axis=0)
        high, low = split(both)
        later = pl.ds(pl.multiple_of(total * LOW + step * 2 * LOW, 2 * LOW), 2 * LOW)
        u_hi[later, :] = high
        u_lo[later, :] = low
        return carry

    lax.fori_loop(0, total // 2, split_factors, 0)
    first_back.wait_recv()
    z0 = returned(0)
    vec_z[...] = z0

    both = stacked(z0)
    send_coeffs(both, 0)
    near = product3(dot_nn, both, diag_hi[...], diag_lo[...])
    q0 = near + far_part(0)
    vec_q[...] = q0
    second_halo = halo_copy(vec_q, 1)
    second_halo.start()

    start_sum(jnp.concatenate([gram(z0, q0), gram(z0, x_ref[...])], axis=1), 0)
    joined[:, halo:] = stacked(q0)
    parts = forward_own()
    middle_sum(0)
    second_halo.wait_recv()
    forward = forward_halo(parts, 1)
    second_back = backward_halo(forward, 1)
    backward_own(forward)
    first_pair = end_sum(0)
    alpha0 = eliminate(first_pair)
    res1 = x_ref[...] - mixed(alpha0, vec_q[...])
    second_back.wait_recv()
    z1 = vec_z[...] - mixed(alpha0, returned(1))

    both = stacked(z1)
    send_coeffs(both, 1)
    start_sum(jnp.concatenate([gram(vec_q[...], z1), gram(z1, res1)], axis=1), 1)
    near = product3(dot_nn, both, diag_hi[...], diag_lo[...])
    middle_sum(1)
    image = near + far_part(1)
    own = gram(z1, image)
    start_sum(jnp.concatenate([own, own], axis=1), 2)
    second_pair = end_sum(1)
    cross, rho1 = second_pair[:, :rhs], second_pair[:, rhs:]
    curve, rho0 = first_pair[:, :rhs], first_pair[:, rhs:]
    beta0_t = eliminate(jnp.concatenate([rho0, rho1], axis=1))
    middle_sum(2)
    search = z1 + mixed(beta0_t, vec_z[...])
    image = image + mixed(beta0_t, vec_q[...])
    sol1 = mixed(alpha0, vec_z[...])
    turned = mixed(beta0_t, cross)
    known = turned + turned.T + gram(mixed(beta0_t, curve), beta0_t)
    own = end_sum(2)[:, :rhs]
    alpha1 = eliminate(jnp.concatenate([own + known, rho1], axis=1))
    sol_ref[...] = sol1 + mixed(alpha1, search)
    res_ref[...] = res1 - mixed(alpha1, image)

    first_halo.wait_send()
    second_halo.wait_send()
    first_back.wait_send()
    second_back.wait_send()
    for call in range(2):
        piece = coef_out.at[call, : (total - 1) * LOW, :]
        pltpu.make_async_copy(piece, piece, coef_send.at[call]).wait()
    for call in range(3):
        piece = sum_row.at[call, : rows - 1]
        pltpu.make_async_copy(piece, piece, row_send.at[call]).wait()
        piece = sum_col.at[call, : cols - 1]
        pltpu.make_async_copy(piece, piece, col_send.at[call]).wait()


def body(rows, cols, right_sides, diag_tiles, low_rank, tile_ranks, inv_factor, sub_sizes):
    rhs, tile = right_sides.shape
    spans, reach, span, _ = inv_factor.shape
    tile_rows, _, groups, _, rank, _ = low_rank.shape
    total = rows * cols
    halo = (reach - 1) * span
    keep = lax.iota(jnp.int32, rank)[None, None, :] < tile_ranks[:, 0, :, None]
    factor = jnp.where(keep[..., None], low_rank[:, 0, :, 1], 0.0).transpose(1, 0, 2, 3)
    ua = factor[:, :, :LOW].reshape(groups, tile_rows * LOW, tile)
    ub = factor[:, :, LOW:].reshape(groups, tile_rows * (rank - LOW), tile)
    anywhere = pl.BlockSpec(memory_space=pl.ANY)
    vmem = pl.BlockSpec(memory_space=pltpu.VMEM)
    dma = pltpu.SemaphoreType.DMA
    out = jax.ShapeDtypeStruct((rhs, tile), F32)
    return pl.pallas_call(
        functools.partial(kernel, rows, cols),
        out_shape=(out, out),
        in_specs=[vmem, anywhere, anywhere, anywhere, anywhere, vmem],
        out_specs=(vmem, vmem),
        scratch_shapes=[
            pltpu.VMEM((spans, span, reach * span), F32),
            pltpu.VMEM((spans, span, reach * span), BF16),
            pltpu.VMEM((spans, span, reach * span), BF16),
            pltpu.VMEM((tile, tile), F32),
            pltpu.VMEM((tile, tile), BF16),
            pltpu.VMEM((tile, tile), BF16),
            pltpu.VMEM((total * LOW, tile), F32),
            pltpu.VMEM((total * (rank - LOW), tile), F32),
            pltpu.VMEM((2 * total * LOW, tile), BF16),
            pltpu.VMEM((2 * total * LOW, tile), BF16),
            pltpu.VMEM((2 * rhs, halo + tile), BF16),
            pltpu.VMEM((2, rhs, halo), F32),
            pltpu.VMEM((2, rhs, halo), F32),
            pltpu.VMEM((2, rhs, halo), F32),
            pltpu.VMEM((rhs, halo + tile), F32),
            pltpu.VMEM((rhs, tile), F32),
            pltpu.VMEM((rhs, tile), F32),
            pltpu.VMEM((2, total * LOW, 2 * rhs), F32),
            pltpu.VMEM((2, total * LOW, 2 * rhs), F32),
            pltpu.VMEM((3, rows, rhs, 2 * rhs), F32),
            pltpu.VMEM((3, cols, rhs, 2 * rhs), F32),
            dma((spans,)), dma, dma((4,)), dma((2, rows)), dma((2, rows)),
            dma((2,)), dma((2,)), dma((2,)), dma((2,)),
            dma((2,)), dma((2,)), dma((3,)), dma((3,)), dma((3,)), dma((3,)),
        ],
        compiler_params=pltpu.CompilerParams(
            collective_id=0, has_side_effects=True, vmem_limit_bytes=60 << 20
        ),
    )(right_sides, diag_tiles, ua, ub, inv_factor, sub_sizes.reshape(1, -1))


def solution(mesh):
    rows, cols = mesh.shape["row"], mesh.shape["col"]
    placed = (
        P(None, ("row", "col")),
        P(("row", "col"), None, None),
        P("row", "col", None, None, None, None),
        P("row", "col", None),
        P(("row", "col"), None, None, None),
        P(),
    )
    return jax.shard_map(
        functools.partial(body, rows, cols),
        mesh=mesh,
        in_specs=placed,
        out_specs=(P(None, ("row", "col")), P(None, ("row", "col"))),
        check_vma=False,
    )
```

```python
import functools

import jax
import jax.numpy as jnp
from jax import lax
from jax.experimental import pallas as pl
from jax.experimental.pallas import tpu as pltpu
from jax.sharding import PartitionSpec as P

MESH = pl.DeviceIdType.MESH
F32 = jnp.float32
BF16 = jnp.bfloat16
LOW = 8
LANES = 128


def split(x):
    high = x.astype(BF16)
    return high, (x - high.astype(F32)).astype(BF16)


def stacked(x):
    high, low = split(x)
    return jnp.concatenate([high, low], axis=0)


def dot_nt(a, b):
    return lax.dot_general(a, b, (((1,), (1,)), ((), ())), preferred_element_type=F32)


def dot_nn(a, b):
    return lax.dot_general(a, b, (((1,), (0,)), ((), ())), preferred_element_type=F32)


def product3(dot, both, high, low):
    rows = both.shape[0] // 2
    first = dot(both, high)
    return first[:rows] + (first[rows:] + dot(both[:rows], low))


def gram(a, b):
    return lax.dot_general(
        a, b, (((1,), (1,)), ((), ())), precision=lax.Precision.HIGHEST, preferred_element_type=F32
    )


def mixed(coeffs, rows):
    return jnp.dot(coeffs, rows, precision=lax.Precision.HIGHEST, preferred_element_type=F32)


def eliminate(work):
    count, width = work.shape
    block = 4
    row_ids = lax.broadcasted_iota(jnp.int32, work.shape, 0)
    for k in range(0, count, block):
        columns = [jnp.broadcast_to(work[:, k + j : k + j + 1], work.shape) for j in range(block)]
        rows = [work[k + i : k + i + 1, :] for i in range(block)]
        heads = [[columns[j][k + i : k + i + 1, :] for j in range(block)] for i in range(block)]
        for i in range(block):
            inverse = 1.0 / heads[i][i]
            rows[i] = rows[i] * inverse
            for j in range(i + 1, block):
                heads[i][j] = heads[i][j] * inverse
            for other in range(block):
                if other != i:
                    factor = heads[other][i]
                    rows[other] = rows[other] - factor * rows[i]
                    for j in range(i + 1, block):
                        heads[other][j] = heads[other][j] - factor * heads[i][j]
        update = columns[0] * rows[0]
        for j in range(1, block):
            update = update + columns[j] * rows[j]
        work = work - update
        for i in range(block):
            work = jnp.where(row_ids == k + i, rows[i], work)
    return work


def solved(work):
    return eliminate(work).T[work.shape[0] :, :]


def kernel(
    rows, cols,
    x_ref, diag_ref, factor_ref, ranks_ref, inv_ref, sizes_ref,
    sol_ref, res_ref,
    inv_f32, inv_hi, inv_lo, diag_f32, diag_hi, diag_lo, ua_f32, ub_f32, u_hi, u_lo,
    factor_f32, pack_a, pack_b, joined, halo_in, back_out, back_in, spread, vec_z, vec_q, coef_out, coef_in, sum_row, sum_col,
    inv_sem, diag_sem, factor_sem, own_sem, u_send, u_recv, halo_send, halo_recv, back_send, back_recv,
    coef_send, coef_recv, row_send, row_recv, col_send, col_recv,
):
    my_row, my_col = lax.axis_index("row"), lax.axis_index("col")
    total = rows * cols
    me = my_row * cols + my_col
    rhs, tile = x_ref.shape
    spans, reach, span, _ = inv_ref.shape
    halo = (reach - 1) * span
    wide = reach * span

    def coords(device):
        return (device // cols, device % cols)

    following = coords((me + 1) % total)
    previous = coords((me + total - 1) % total)

    barrier = pltpu.get_barrier_semaphore()

    def greet(step, carry):
        pl.semaphore_signal(
            barrier, inc=1, device_id=coords((me + step) % total), device_id_type=MESH
        )
        return carry

    lax.fori_loop(1, total, greet, 0)

    factor_copy = pltpu.make_async_copy(factor_ref, factor_f32, factor_sem)
    factor_copy.start()
    for a in range(spans):
        for t in range(reach):
            copy = pltpu.make_async_copy(
                inv_ref.at[a, t],
                inv_f32.at[a, :, (reach - 1 - t) * span : (reach - t) * span],
                inv_sem.at[a],
            )
            copy.start()
    diag_copy = pltpu.make_async_copy(diag_ref.at[0], diag_f32, diag_sem)
    diag_copy.start()
    groups = rows
    rank = factor_ref.shape[0] // (cols * groups * 2 * (tile // LANES))
    tail = rank - LOW
    step_rows = 2 * (tile // LANES)

    def at_rows(ref, index, size):
        return ref.at[pl.ds(pl.multiple_of(index * size, size), size), :]

    def take(base, side, first, size, limit):
        ids = first + lax.broadcasted_iota(jnp.int32, (size, LANES), 0)
        pieces = [
            factor_f32[pl.ds(base + first * step_rows + 2 * i + side, size, stride=step_rows), :]
            for i in range(tile // LANES)
        ]
        return jnp.concatenate([jnp.where(ids < limit, piece, 0.0) for piece in pieces], axis=1)

    factor_copy.wait()

    def pack(k, carry):
        for a in range(cols):
            base = (a * groups + k) * rank * step_rows
            limit = ranks_ref[a, 0, k]
            pack_a[k, a * LOW : (a + 1) * LOW, :] = take(base, 1, 0, LOW, limit)
            pack_b[k, a * tail : (a + 1) * tail, :] = take(base, 1, LOW, tail, limit)
        base = (my_col * groups + k) * rank * step_rows
        where = pl.ds(pl.multiple_of((k * cols + my_col) * LOW, LOW), LOW)
        ua_f32[where, :] = take(base, 0, 0, LOW, ranks_ref[my_col, 0, k])
        return carry

    lax.fori_loop(0, groups, pack, 0)
    own_b = pltpu.make_async_copy(
        pack_b.at[my_row], at_rows(ub_f32, my_row, cols * tail), own_sem.at[0]
    )
    own_b.start()

    def own_a(step):
        a = (my_col + step) % cols
        return pltpu.make_async_copy(
            at_rows(pack_a.at[my_row], a, LOW), at_rows(ua_f32, my_row * cols + a, LOW), own_sem.at[1]
        )

    for step in range(1, cols):
        own_a(step).start()
    pl.semaphore_wait(barrier, total - 1)

    def remote(src, dst, send, recv, device):
        return pltpu.make_async_remote_copy(
            src_ref=src, dst_ref=dst, send_sem=send, recv_sem=recv, device_id=device,
            device_id_type=MESH,
        )

    def halo_copy(src, call):
        return remote(
            src.at[:, tile - halo : tile], halo_in.at[call], halo_send.at[call],
            halo_recv.at[call], following,
        )

    first_halo = halo_copy(x_ref, 0)
    first_halo.start()

    def send_factors(step, carry):
        peer = (my_row + step) % rows
        for turn in range(1, cols):
            a = (my_col + turn) % cols
            remote(at_rows(pack_a.at[peer], a, LOW), at_rows(ua_f32, my_row * cols + a, LOW),
                   u_send.at[0], u_recv.at[0], (peer, my_col)).start()
        remote(pack_b.at[peer], at_rows(ub_f32, my_row, cols * tail), u_send.at[1], u_recv.at[1],
               (peer, my_col)).start()
        return carry

    lax.fori_loop(1, rows, send_factors, 0)

    subs = sizes_ref.shape[1]
    sizes = jnp.broadcast_to(sizes_ref[...].astype(F32), (subs, subs))
    down = lax.broadcasted_iota(jnp.int32, (subs, subs), 0)
    across = lax.broadcasted_iota(jnp.int32, (subs, subs), 1)
    opening = jnp.sum(jnp.where(across < down, sizes, 0.0), axis=1, keepdims=True)
    behind = (reach - 1) - lax.broadcasted_iota(jnp.int32, (1, wide), 1) // span
    behind = behind.astype(F32)

    vec = x_ref[...]
    joined[:, halo:] = stacked(vec)

    for a in range(spans):
        for t in range(reach):
            pltpu.make_async_copy(
                inv_ref.at[a, t], inv_f32.at[a, :, t * span : (t + 1) * span], inv_sem.at[a]
            ).wait()
        number = (me * spans + a).astype(F32)
        start = jnp.max(jnp.where(opening <= number, opening, 0.0), axis=0, keepdims=True)
        mask = jnp.where(behind <= number - start, 1.0, 0.0)
        high, low = split(inv_f32[a] * mask)
        inv_hi[a] = high
        inv_lo[a] = low

    def forward_own():
        parts = []
        for a in range(spans):
            skip = max(0, halo - a * span)
            parts.append(product3(
                dot_nt, joined[:, a * span + skip : a * span + wide],
                inv_hi[a, :, skip:], inv_lo[a, :, skip:],
            ))
        return parts

    def forward_halo(parts, call):
        joined[:, :halo] = stacked(halo_in[call])
        out = []
        for a in range(spans):
            skip = max(0, halo - a * span)
            part = parts[a]
            if skip:
                part = part + product3(
                    dot_nt, joined[:, a * span : halo], inv_hi[a, :, :skip], inv_lo[a, :, :skip]
                )
            out.append(stacked(part))
        return out

    def backward_halo(forward, call):
        spread[:, :halo] = jnp.zeros((rhs, halo), F32)
        for a in range(spans):
            skip = max(0, halo - a * span)
            if skip:
                spread[:, a * span : halo] += product3(
                    dot_nn, forward[a], inv_hi[a, :, :skip], inv_lo[a, :, :skip]
                )
        back_out[call] = spread[:, :halo]
        copy = remote(back_out.at[call], back_in.at[call], back_send.at[call],
                      back_recv.at[call], previous)
        copy.start()
        return copy

    def backward_own(forward):
        spread[:, halo:] = jnp.zeros((rhs, tile), F32)
        for a in range(spans):
            skip = max(0, halo - a * span)
            spread[:, a * span + skip : a * span + wide] += product3(
                dot_nn, forward[a], inv_hi[a, :, skip:], inv_lo[a, :, skip:]
            )

    def returned(call):
        spread[:, halo + tile - halo :] += back_in[call]
        return spread[:, halo:]

    def send_coeffs(both, call):
        wide_part = dot_nt(u_hi[...], both)
        coeffs = wide_part[:, :rhs] + (wide_part[:, rhs:] + dot_nt(u_lo[...], both[:rhs]))
        half = coeffs.shape[0] // 2
        coef_out[call, :, :rhs] = coeffs[:half]
        coef_out[call, :, rhs:] = coeffs[half:]

        def send(peer_row, peer_col):
            remote(at_rows(coef_out.at[call], peer_row * cols + peer_col, LOW),
                   at_rows(coef_in.at[call], me, LOW),
                   coef_send.at[call], coef_recv.at[call], (peer_row, peer_col)).start()

        def send_row(step, carry):
            peer_row = (my_row + step) % rows
            for turn in range(cols):
                send(peer_row, (my_col + turn) % cols)
            return carry

        lax.fori_loop(1, rows, send_row, 0)
        for turn in range(1, cols):
            send(my_row, (my_col + turn) % cols)
        pltpu.make_async_copy(
            at_rows(coef_out.at[call], me, LOW), at_rows(coef_in.at[call], me, LOW), own_sem.at[2 + call]
        ).start()

    def wait_coeffs(call):
        piece = coef_out.at[call, : (total - 1) * LOW, :]
        pltpu.make_async_copy(piece, piece, coef_recv.at[call]).wait()
        pltpu.make_async_copy(
            at_rows(coef_out.at[call], me, LOW), at_rows(coef_in.at[call], me, LOW), own_sem.at[2 + call]
        ).wait()
        turned = coef_in[call].T
        return stacked(jnp.concatenate([turned[:rhs], turned[rhs:]], axis=1))

    def far_part(call):
        return product3(dot_nn, wait_coeffs(call), u_hi[...], u_lo[...])

    heights = (rhs, rhs, rhs // 2)

    def start_sum(value, call):
        high = heights[call]
        sum_row[call, my_row, :high] = value
        for step in range(1, rows):
            mine = sum_row.at[call, my_row, :high]
            remote(mine, mine, row_send.at[call],
                   row_recv.at[call], ((my_row + step) % rows, my_col)).start()

    def middle_sum(call):
        high = heights[call]
        piece = sum_row.at[call, : rows - 1, :high]
        pltpu.make_async_copy(piece, piece, row_recv.at[call]).wait()
        sum_col[call, my_col, :high] = jnp.sum(sum_row[call, :, :high], axis=0)
        for step in range(1, cols):
            mine = sum_col.at[call, my_col, :high]
            remote(mine, mine, col_send.at[call],
                   col_recv.at[call], (my_row, (my_col + step) % cols)).start()

    def end_sum(call):
        high = heights[call]
        piece = sum_col.at[call, : cols - 1, :high]
        pltpu.make_async_copy(piece, piece, col_recv.at[call]).wait()
        return jnp.sum(sum_col[call, :, :high], axis=0)

    parts = forward_own()
    first_halo.wait_recv()
    forward = forward_halo(parts, 0)
    first_back = backward_halo(forward, 0)
    backward_own(forward)
    diag_copy.wait()

    def split_diag(step, carry):
        where = pl.ds(pl.multiple_of(step * span, span), span)
        high, low = split(diag_f32[where, :])
        diag_hi[where, :] = high
        diag_lo[where, :] = low
        return carry

    lax.fori_loop(0, tile // span, split_diag, 0)
    own_b.wait()
    own_piece = ua_f32.at[: (cols - 1) * LOW, :]
    pltpu.make_async_copy(own_piece, own_piece, own_sem.at[1]).wait()
    piece_a = ua_f32.at[: (rows - 1) * (cols - 1) * LOW, :]
    piece_b = ub_f32.at[: (rows - 1) * cols * tail, :]
    pltpu.make_async_copy(piece_a, piece_a, u_recv.at[0]).wait()
    pltpu.make_async_copy(piece_b, piece_b, u_recv.at[1]).wait()
    upper = lax.broadcasted_iota(jnp.int32, (LOW, tile), 0) < tail

    def split_factors(step, carry):
        where = pl.ds(pl.multiple_of(step * 2 * LOW, 2 * LOW), 2 * LOW)
        high, low = split(ua_f32[where, :])
        u_hi[where, :] = high
        u_lo[where, :] = low
        pair = ub_f32[pl.ds(pl.multiple_of(step * LOW, LOW), LOW), :]
        other = jnp.concatenate([pair[tail:], pair[:tail]], axis=0)
        both = jnp.concatenate([jnp.where(upper, pair, 0.0), jnp.where(upper, other, 0.0)], axis=0)
        high, low = split(both)
        later = pl.ds(pl.multiple_of(total * LOW + step * 2 * LOW, 2 * LOW), 2 * LOW)
        u_hi[later, :] = high
        u_lo[later, :] = low
        return carry

    lax.fori_loop(0, total // 2, split_factors, 0)
    first_back.wait_recv()
    z0 = returned(0)
    vec_z[...] = z0

    both = stacked(z0)
    send_coeffs(both, 0)
    near = product3(dot_nn, both, diag_hi[...], diag_lo[...])
    q0 = near + far_part(0)
    vec_q[...] = q0
    second_halo = halo_copy(vec_q, 1)
    second_halo.start()

    start_sum(jnp.concatenate([gram(z0, q0), gram(z0, x_ref[...])], axis=1), 0)
    joined[:, halo:] = stacked(q0)
    parts = forward_own()
    middle_sum(0)
    second_halo.wait_recv()
    forward = forward_halo(parts, 1)
    second_back = backward_halo(forward, 1)
    backward_own(forward)
    first_pair = end_sum(0)
    alpha0 = solved(first_pair)
    res1 = x_ref[...] - mixed(alpha0, vec_q[...])
    second_back.wait_recv()
    z1 = vec_z[...] - mixed(alpha0, returned(1))

    both = stacked(z1)
    send_coeffs(both, 1)
    start_sum(jnp.concatenate([gram(vec_q[...], z1), gram(z1, res1)], axis=1), 1)
    near = product3(dot_nn, both, diag_hi[...], diag_lo[...])
    curve, rho0 = first_pair[:, :rhs], first_pair[:, rhs:]
    square = (rhs, rhs)
    identity = (
        lax.broadcasted_iota(jnp.int32, square, 0) == lax.broadcasted_iota(jnp.int32, square, 1)
    ).astype(F32)
    inverse = eliminate(jnp.concatenate([rho0, identity], axis=1))[:, rhs:]
    sol1 = mixed(alpha0, vec_z[...])
    middle_sum(1)
    image = near + far_part(1)
    own = gram(z1, image)
    start_sum(jnp.concatenate([own[: rhs // 2], own[rhs // 2 :]], axis=1), 2)
    second_pair = end_sum(1)
    cross, rho1 = second_pair[:, :rhs], second_pair[:, rhs:]
    beta0_t = mixed(inverse, rho1).T
    middle_sum(2)
    search = z1 + mixed(beta0_t, vec_z[...])
    image = image + mixed(beta0_t, vec_q[...])
    turned = mixed(beta0_t, cross)
    known = turned + turned.T + gram(mixed(beta0_t, curve), beta0_t)
    halves = end_sum(2)
    own = jnp.concatenate([halves[:, :rhs], halves[:, rhs:]], axis=0)
    alpha1 = solved(jnp.concatenate([own + known, rho1], axis=1))
    sol_ref[...] = sol1 + mixed(alpha1, search)
    res_ref[...] = res1 - mixed(alpha1, image)

    pltpu.make_async_copy(piece_a, piece_a, u_send.at[0]).wait()
    pltpu.make_async_copy(piece_b, piece_b, u_send.at[1]).wait()
    first_halo.wait_send()
    second_halo.wait_send()
    first_back.wait_send()
    second_back.wait_send()
    for call in range(2):
        piece = coef_out.at[call, : (total - 1) * LOW, :]
        pltpu.make_async_copy(piece, piece, coef_send.at[call]).wait()
    for call in range(3):
        piece = sum_row.at[call, : rows - 1, : heights[call]]
        pltpu.make_async_copy(piece, piece, row_send.at[call]).wait()
        piece = sum_col.at[call, : cols - 1, : heights[call]]
        pltpu.make_async_copy(piece, piece, col_send.at[call]).wait()


def body(rows, cols, right_sides, diag_tiles, low_rank, tile_ranks, inv_factor, sub_sizes):
    rhs, tile = right_sides.shape
    spans, reach, span, _ = inv_factor.shape
    tile_rows, _, groups, _, rank, _ = low_rank.shape
    total = rows * cols
    halo = (reach - 1) * span
    pieces = tile // LANES
    factor = low_rank.reshape(tile_rows, groups, 2, rank, pieces, LANES)
    factor = factor.transpose(0, 1, 3, 4, 2, 5).reshape(-1, LANES)
    anywhere = pl.BlockSpec(memory_space=pl.ANY)
    vmem = pl.BlockSpec(memory_space=pltpu.VMEM)
    dma = pltpu.SemaphoreType.DMA
    out = jax.ShapeDtypeStruct((rhs, tile), F32)
    return pl.pallas_call(
        functools.partial(kernel, rows, cols),
        out_shape=(out, out),
        in_specs=[vmem, anywhere, anywhere, pl.BlockSpec(memory_space=pltpu.SMEM), anywhere, vmem],
        out_specs=(vmem, vmem),
        scratch_shapes=[
            pltpu.VMEM((spans, span, reach * span), F32),
            pltpu.VMEM((spans, span, reach * span), BF16),
            pltpu.VMEM((spans, span, reach * span), BF16),
            pltpu.VMEM((tile, tile), F32),
            pltpu.VMEM((tile, tile), BF16),
            pltpu.VMEM((tile, tile), BF16),
            pltpu.VMEM((total * LOW, tile), F32),
            pltpu.VMEM((total * (rank - LOW), tile), F32),
            pltpu.VMEM((2 * total * LOW, tile), BF16),
            pltpu.VMEM((2 * total * LOW, tile), BF16),
            pltpu.VMEM(factor.shape, F32),
            pltpu.VMEM((groups, tile_rows * LOW, tile), F32),
            pltpu.VMEM((groups, tile_rows * (rank - LOW), tile), F32),
            pltpu.VMEM((2 * rhs, halo + tile), BF16),
            pltpu.VMEM((2, rhs, halo), F32),
            pltpu.VMEM((2, rhs, halo), F32),
            pltpu.VMEM((2, rhs, halo), F32),
            pltpu.VMEM((rhs, halo + tile), F32),
            pltpu.VMEM((rhs, tile), F32),
            pltpu.VMEM((rhs, tile), F32),
            pltpu.VMEM((2, total * LOW, 2 * rhs), F32),
            pltpu.VMEM((2, total * LOW, 2 * rhs), F32),
            pltpu.VMEM((3, rows, rhs, 2 * rhs), F32),
            pltpu.VMEM((3, cols, rhs, 2 * rhs), F32),
            dma((spans,)), dma, dma, dma((4,)), dma((2,)), dma((2,)),
            dma((2,)), dma((2,)), dma((2,)), dma((2,)),
            dma((2,)), dma((2,)), dma((3,)), dma((3,)), dma((3,)), dma((3,)),
        ],
        compiler_params=pltpu.CompilerParams(
            collective_id=0, has_side_effects=True, vmem_limit_bytes=60 << 20
        ),
    )(right_sides, diag_tiles, factor, tile_ranks, inv_factor, sub_sizes.reshape(1, -1))


def solution(mesh):
    rows, cols = mesh.shape["row"], mesh.shape["col"]
    placed = (
        P(None, ("row", "col")),
        P(("row", "col"), None, None),
        P("row", "col", None, None, None, None),
        P("row", "col", None),
        P(("row", "col"), None, None, None),
        P(),
    )
    return jax.shard_map(
        functools.partial(body, rows, cols),
        mesh=mesh,
        in_specs=placed,
        out_specs=(P(None, ("row", "col")), P(None, ("row", "col"))),
        check_vma=False,
    )
```

```python
import functools
import math

import jax
import jax.numpy as jnp
from jax import lax
from jax.experimental import pallas as pl
from jax.experimental.pallas import tpu as pltpu
from jax.sharding import PartitionSpec as P

MESH = pl.DeviceIdType.MESH
F32 = jnp.float32
BF16 = jnp.bfloat16
LOW = 8
LANES = 128


def split(x):
    high = x.astype(BF16)
    return high, (x - high.astype(F32)).astype(BF16)


def stacked(x):
    high, low = split(x)
    return jnp.concatenate([high, low], axis=0)


def dot_nt(a, b):
    return lax.dot_general(a, b, (((1,), (1,)), ((), ())), preferred_element_type=F32)


def dot_nn(a, b):
    return lax.dot_general(a, b, (((1,), (0,)), ((), ())), preferred_element_type=F32)


def product3(dot, both, high, low):
    rows = both.shape[0] // 2
    first = dot(both, high)
    return first[:rows] + (first[rows:] + dot(both[:rows], low))


def gram(a, b):
    return lax.dot_general(
        a, b, (((1,), (1,)), ((), ())), precision=lax.Precision.HIGHEST, preferred_element_type=F32
    )


def mixed(coeffs, rows):
    return jnp.dot(coeffs, rows, precision=lax.Precision.HIGHEST, preferred_element_type=F32)


def eliminate(work):
    count, width = work.shape
    block = 4
    row_ids = lax.broadcasted_iota(jnp.int32, work.shape, 0)
    for k in range(0, count, block):
        columns = [jnp.broadcast_to(work[:, k + j : k + j + 1], work.shape) for j in range(block)]
        rows = [work[k + i : k + i + 1, :] for i in range(block)]
        heads = [[columns[j][k + i : k + i + 1, :] for j in range(block)] for i in range(block)]
        for i in range(block):
            inverse = 1.0 / heads[i][i]
            rows[i] = rows[i] * inverse
            for j in range(i + 1, block):
                heads[i][j] = heads[i][j] * inverse
            for other in range(block):
                if other != i:
                    factor = heads[other][i]
                    rows[other] = rows[other] - factor * rows[i]
                    for j in range(i + 1, block):
                        heads[other][j] = heads[other][j] - factor * heads[i][j]
        update = columns[0] * rows[0]
        for j in range(1, block):
            update = update + columns[j] * rows[j]
        work = work - update
        for i in range(block):
            work = jnp.where(row_ids == k + i, rows[i], work)
    return work


def solved(work):
    return eliminate(work).T[work.shape[0] :, :]


def kernel(
    rows, cols,
    x_ref, diag_ref, factor_ref, ranks_ref, inv_ref, sizes_ref,
    sol_ref, res_ref,
    inv_f32, inv_hi, inv_lo, diag_f32, diag_hi, diag_lo, u_f32, u_hi, u_lo,
    factor_f32, packed, joined, halo_in, back_out, back_in, spread, vec_z, vec_q, coef_out, coef_in, sum_row, sum_col,
    inv_sem, diag_sem, factor_sem, own_sem, u_send, u_recv, halo_send, halo_recv, back_send, back_recv,
    coef_send, coef_recv, row_send, row_recv, col_send, col_recv,
):
    my_row, my_col = lax.axis_index("row"), lax.axis_index("col")
    total = rows * cols
    me = my_row * cols + my_col
    rhs, tile = x_ref.shape
    spans, reach, span, _ = inv_ref.shape
    halo = (reach - 1) * span
    wide = reach * span

    def coords(device):
        return (device // cols, device % cols)

    following = coords((me + 1) % total)
    previous = coords((me + total - 1) % total)

    barrier = pltpu.get_barrier_semaphore()

    def greet(step, carry):
        pl.semaphore_signal(
            barrier, inc=1, device_id=coords((me + step) % total), device_id_type=MESH
        )
        return carry

    lax.fori_loop(1, total, greet, 0)

    factor_copy = pltpu.make_async_copy(factor_ref, factor_f32, factor_sem)
    factor_copy.start()
    for a in range(spans):
        for t in range(reach):
            copy = pltpu.make_async_copy(
                inv_ref.at[a, t],
                inv_f32.at[a, :, (reach - 1 - t) * span : (reach - t) * span],
                inv_sem.at[a],
            )
            copy.start()
    diag_copy = pltpu.make_async_copy(diag_ref.at[0], diag_f32, diag_sem)
    diag_copy.start()
    groups = rows
    rank = factor_ref.shape[0] // (cols * groups * 2 * (tile // LANES))
    tail = rank - LOW
    step_rows = 2 * (tile // LANES)

    def at_rows(ref, index, size):
        return ref.at[pl.ds(pl.multiple_of(index * size, size), size), :]

    def take(base, side, first, size, limit):
        ids = first + lax.broadcasted_iota(jnp.int32, (size, LANES), 0)
        pieces = [
            factor_f32[pl.ds(base + first * step_rows + 2 * i + side, size, stride=step_rows), :]
            for i in range(tile // LANES)
        ]
        return jnp.concatenate([jnp.where(ids < limit, piece, 0.0) for piece in pieces], axis=1)

    factor_copy.wait()

    def block(base, side, limit):
        rest = take(base, side, LOW, tail, limit)
        rest = jnp.concatenate([rest[:, : tile // 2], rest[:, tile // 2 :]], axis=0)
        return take(base, side, 0, LOW, limit), rest

    def pack(k, carry):
        for a in range(cols):
            base = (a * groups + k) * rank * step_rows
            first, rest = block(base, 1, ranks_ref[a, 0, k])
            packed[k, a * LOW : (a + 1) * LOW, :tile] = first
            packed[k, a * LOW : (a + 1) * LOW, tile:] = rest
        base = (my_col * groups + k) * rank * step_rows
        where = pl.ds(pl.multiple_of((k * cols + my_col) * LOW, LOW), LOW)
        first, rest = block(base, 0, ranks_ref[my_col, 0, k])
        u_f32[where, :tile] = first
        u_f32[where, tile:] = rest
        return carry

    lax.fori_loop(0, groups, pack, 0)

    for turn in range(1, cols):
        a = (my_col + turn) % cols
        pltpu.make_async_copy(
            at_rows(packed.at[my_row], a, LOW), at_rows(u_f32, my_row * cols + a, LOW), own_sem.at[1]
        ).start()
    pl.semaphore_wait(barrier, total - 1)

    def remote(src, dst, send, recv, device):
        return pltpu.make_async_remote_copy(
            src_ref=src, dst_ref=dst, send_sem=send, recv_sem=recv, device_id=device,
            device_id_type=MESH,
        )

    def halo_copy(src, call):
        return remote(
            src.at[:, tile - halo : tile], halo_in.at[call], halo_send.at[call],
            halo_recv.at[call], following,
        )

    first_halo = halo_copy(x_ref, 0)
    first_halo.start()

    def send_factors(step, carry):
        peer = (my_row + step) % rows
        for turn in range(1, cols):
            a = (my_col + turn) % cols
            remote(at_rows(packed.at[peer], a, LOW), at_rows(u_f32, my_row * cols + a, LOW),
                   u_send, u_recv, (peer, my_col)).start()
        return carry

    lax.fori_loop(1, rows, send_factors, 0)

    subs = sizes_ref.shape[1]
    sizes = jnp.broadcast_to(sizes_ref[...].astype(F32), (subs, subs))
    down = lax.broadcasted_iota(jnp.int32, (subs, subs), 0)
    across = lax.broadcasted_iota(jnp.int32, (subs, subs), 1)
    opening = jnp.sum(jnp.where(across < down, sizes, 0.0), axis=1, keepdims=True)
    behind = (reach - 1) - lax.broadcasted_iota(jnp.int32, (1, wide), 1) // span
    behind = behind.astype(F32)

    vec = x_ref[...]
    joined[:, halo:] = stacked(vec)

    for a in range(spans):
        for t in range(reach):
            pltpu.make_async_copy(
                inv_ref.at[a, t], inv_f32.at[a, :, t * span : (t + 1) * span], inv_sem.at[a]
            ).wait()
        number = (me * spans + a).astype(F32)
        start = jnp.max(jnp.where(opening <= number, opening, 0.0), axis=0, keepdims=True)
        mask = jnp.where(behind <= number - start, 1.0, 0.0)
        high, low = split(inv_f32[a] * mask)
        inv_hi[a] = high
        inv_lo[a] = low

    def forward_own():
        parts = []
        for a in range(spans):
            skip = max(0, halo - a * span)
            parts.append(product3(
                dot_nt, joined[:, a * span + skip : a * span + wide],
                inv_hi[a, :, skip:], inv_lo[a, :, skip:],
            ))
        return parts

    def forward_halo(parts, call):
        joined[:, :halo] = stacked(halo_in[call])
        out = []
        for a in range(spans):
            skip = max(0, halo - a * span)
            part = parts[a]
            if skip:
                part = part + product3(
                    dot_nt, joined[:, a * span : halo], inv_hi[a, :, :skip], inv_lo[a, :, :skip]
                )
            out.append(stacked(part))
        return out

    def backward_halo(forward, call):
        spread[:, :halo] = jnp.zeros((rhs, halo), F32)
        for a in range(spans):
            skip = max(0, halo - a * span)
            if skip:
                spread[:, a * span : halo] += product3(
                    dot_nn, forward[a], inv_hi[a, :, :skip], inv_lo[a, :, :skip]
                )
        back_out[call] = spread[:, :halo]
        copy = remote(back_out.at[call], back_in.at[call], back_send.at[call],
                      back_recv.at[call], previous)
        copy.start()
        return copy

    def backward_own(forward):
        spread[:, halo:] = jnp.zeros((rhs, tile), F32)
        for a in range(spans):
            skip = max(0, halo - a * span)
            spread[:, a * span + skip : a * span + wide] += product3(
                dot_nn, forward[a], inv_hi[a, :, skip:], inv_lo[a, :, skip:]
            )

    def returned(call):
        spread[:, halo + tile - halo :] += back_in[call]
        return spread[:, halo:]

    def send_coeffs(both, call):
        wide_part = dot_nt(u_hi[...], both)
        coeffs = wide_part[:, :rhs] + (wide_part[:, rhs:] + dot_nt(u_lo[...], both[:rhs]))
        half = coeffs.shape[0] // 2
        coef_out[call, :, :rhs] = coeffs[:half]
        coef_out[call, :, rhs:] = coeffs[half:]

        def send(peer_row, peer_col):
            remote(at_rows(coef_out.at[call], peer_row * cols + peer_col, LOW),
                   at_rows(coef_in.at[call], me, LOW),
                   coef_send.at[call], coef_recv.at[call], (peer_row, peer_col)).start()

        def send_row(step, carry):
            peer_row = (my_row + step) % rows
            for turn in range(cols):
                send(peer_row, (my_col + turn) % cols)
            return carry

        lax.fori_loop(1, rows, send_row, 0)
        for turn in range(1, cols):
            send(my_row, (my_col + turn) % cols)
        pltpu.make_async_copy(
            at_rows(coef_out.at[call], me, LOW), at_rows(coef_in.at[call], me, LOW), own_sem.at[2 + call]
        ).start()

    def wait_coeffs(call):
        piece = coef_out.at[call, : (total - 1) * LOW, :]
        pltpu.make_async_copy(piece, piece, coef_recv.at[call]).wait()
        pltpu.make_async_copy(
            at_rows(coef_out.at[call], me, LOW), at_rows(coef_in.at[call], me, LOW), own_sem.at[2 + call]
        ).wait()
        turned = coef_in[call].T
        return stacked(jnp.concatenate([turned[:rhs], turned[rhs:]], axis=1))

    def far_part(call):
        return product3(dot_nn, wait_coeffs(call), u_hi[...], u_lo[...])

    heights = (rhs // 2, rhs, rhs // 2, rhs // 2)

    def start_sum(value, call):
        high = heights[call]
        sum_row[call, my_row, :high] = value
        for step in range(1, rows):
            mine = sum_row.at[call, my_row, :high]
            remote(mine, mine, row_send.at[call],
                   row_recv.at[call], ((my_row + step) % rows, my_col)).start()

    def middle_sum(call):
        high = heights[call]
        piece = sum_row.at[call, : rows - 1, :high]
        pltpu.make_async_copy(piece, piece, row_recv.at[call]).wait()
        sum_col[call, my_col, :high] = jnp.sum(sum_row[call, :, :high], axis=0)
        for step in range(1, cols):
            mine = sum_col.at[call, my_col, :high]
            remote(mine, mine, col_send.at[call],
                   col_recv.at[call], (my_row, (my_col + step) % cols)).start()

    def end_sum(call):
        high = heights[call]
        piece = sum_col.at[call, : cols - 1, :high]
        pltpu.make_async_copy(piece, piece, col_recv.at[call]).wait()
        return jnp.sum(sum_col[call, :, :high], axis=0)

    def folded(square):
        return jnp.concatenate([square[: rhs // 2], square[rhs // 2 :]], axis=1)

    def unfolded(halves):
        return jnp.concatenate([halves[:, :rhs], halves[:, rhs:]], axis=0)

    parts = forward_own()
    first_halo.wait_recv()
    forward = forward_halo(parts, 0)
    first_back = backward_halo(forward, 0)
    backward_own(forward)
    diag_copy.wait()

    def split_diag(step, carry):
        where = pl.ds(pl.multiple_of(step * span, span), span)
        high, low = split(diag_f32[where, :])
        diag_hi[where, :] = high
        diag_lo[where, :] = low
        return carry

    lax.fori_loop(0, tile // span, split_diag, 0)
    own_piece = u_f32.at[: (cols - 1) * LOW, :]
    pltpu.make_async_copy(own_piece, own_piece, own_sem.at[1]).wait()
    others = u_f32.at[: (rows - 1) * (cols - 1) * LOW, :]
    pltpu.make_async_copy(others, others, u_recv).wait()
    empty = jnp.zeros((LOW - tail, tile), F32)

    def split_factors(step, carry):
        where = pl.ds(pl.multiple_of(step * 2 * LOW, 2 * LOW), 2 * LOW)
        high, low = split(u_f32[where, :tile])
        u_hi[where, :] = high
        u_lo[where, :] = low
        rest = u_f32[where, tile:]
        parts = []
        for first in (0, LOW):
            parts.append(jnp.concatenate(
                [rest[first : first + tail], rest[first + tail : first + 2 * tail]], axis=1
            ))
            parts.append(empty)
        high, low = split(jnp.concatenate(parts, axis=0))
        later = pl.ds(pl.multiple_of(total * LOW + step * 2 * LOW, 2 * LOW), 2 * LOW)
        u_hi[later, :] = high
        u_lo[later, :] = low
        return carry

    lax.fori_loop(0, total // 2, split_factors, 0)
    first_back.wait_recv()
    z0 = returned(0)
    vec_z[...] = z0

    both = stacked(z0)
    send_coeffs(both, 0)
    start_sum(folded(gram(z0, x_ref[...])), 3)
    near = product3(dot_nn, both, diag_hi[...], diag_lo[...])
    middle_sum(3)
    q0 = near + far_part(0)
    vec_q[...] = q0
    second_halo = halo_copy(vec_q, 1)
    second_halo.start()

    start_sum(folded(gram(z0, q0)), 0)
    joined[:, halo:] = stacked(q0)
    parts = forward_own()
    middle_sum(0)
    second_halo.wait_recv()
    forward = forward_halo(parts, 1)
    second_back = backward_halo(forward, 1)
    backward_own(forward)
    rho0 = unfolded(end_sum(3))
    curve = unfolded(end_sum(0))
    alpha0 = solved(jnp.concatenate([curve, rho0], axis=1))
    res1 = x_ref[...] - mixed(alpha0, vec_q[...])
    second_back.wait_recv()
    z1 = vec_z[...] - mixed(alpha0, returned(1))

    both = stacked(z1)
    send_coeffs(both, 1)
    start_sum(jnp.concatenate([gram(vec_q[...], z1), gram(z1, res1)], axis=1), 1)
    near = product3(dot_nn, both, diag_hi[...], diag_lo[...])
    square = (rhs, rhs)
    identity = (
        lax.broadcasted_iota(jnp.int32, square, 0) == lax.broadcasted_iota(jnp.int32, square, 1)
    ).astype(F32)
    inverse = eliminate(jnp.concatenate([rho0, identity], axis=1))[:, rhs:]
    sol1 = mixed(alpha0, vec_z[...])
    middle_sum(1)
    image = near + far_part(1)
    own = gram(z1, image)
    start_sum(folded(own), 2)
    second_pair = end_sum(1)
    cross, rho1 = second_pair[:, :rhs], second_pair[:, rhs:]
    beta0_t = mixed(inverse, rho1).T
    middle_sum(2)
    search = z1 + mixed(beta0_t, vec_z[...])
    image = image + mixed(beta0_t, vec_q[...])
    turned = mixed(beta0_t, cross)
    known = turned + turned.T + gram(mixed(beta0_t, curve), beta0_t)
    own = unfolded(end_sum(2))
    alpha1 = solved(jnp.concatenate([own + known, rho1], axis=1))
    sol_ref[...] = sol1 + mixed(alpha1, search)
    res_ref[...] = res1 - mixed(alpha1, image)

    pltpu.make_async_copy(others, others, u_send).wait()
    first_halo.wait_send()
    second_halo.wait_send()
    first_back.wait_send()
    second_back.wait_send()
    for call in range(2):
        piece = coef_out.at[call, : (total - 1) * LOW, :]
        pltpu.make_async_copy(piece, piece, coef_send.at[call]).wait()
    for call in range(4):
        piece = sum_row.at[call, : rows - 1, : heights[call]]
        pltpu.make_async_copy(piece, piece, row_send.at[call]).wait()
        piece = sum_col.at[call, : cols - 1, : heights[call]]
        pltpu.make_async_copy(piece, piece, col_send.at[call]).wait()


def body(rows, cols, right_sides, diag_tiles, low_rank, tile_ranks, inv_factor, sub_sizes):
    rhs, tile = right_sides.shape
    spans, reach, span, _ = inv_factor.shape
    tile_rows, _, groups, _, rank, _ = low_rank.shape
    total = rows * cols
    halo = (reach - 1) * span
    pieces = tile // LANES
    factor = low_rank.reshape(tile_rows, groups, 2, rank, pieces, LANES)
    factor = factor.transpose(0, 1, 3, 4, 2, 5).reshape(-1, LANES)
    in_hbm = pl.BlockSpec(memory_space=pltpu.HBM)
    vmem = pl.BlockSpec(memory_space=pltpu.VMEM)
    dma = pltpu.SemaphoreType.DMA
    out = jax.ShapeDtypeStruct((rhs, tile), F32)
    buffers = [
        pltpu.VMEM((spans, span, reach * span), F32),
        pltpu.VMEM((spans, span, reach * span), BF16),
        pltpu.VMEM((spans, span, reach * span), BF16),
        pltpu.VMEM((tile, tile), F32),
        pltpu.VMEM((tile, tile), BF16),
        pltpu.VMEM((tile, tile), BF16),
        pltpu.VMEM((total * LOW, tile + tile // 2), F32),
        pltpu.VMEM((2 * total * LOW, tile), BF16),
        pltpu.VMEM((2 * total * LOW, tile), BF16),
        pltpu.VMEM(factor.shape, F32),
        pltpu.VMEM((groups, tile_rows * LOW, tile + tile // 2), F32),
        pltpu.VMEM((2 * rhs, halo + tile), BF16),
        pltpu.VMEM((2, rhs, halo), F32),
        pltpu.VMEM((2, rhs, halo), F32),
        pltpu.VMEM((2, rhs, halo), F32),
        pltpu.VMEM((rhs, halo + tile), F32),
        pltpu.VMEM((rhs, tile), F32),
        pltpu.VMEM((rhs, tile), F32),
        pltpu.VMEM((2, total * LOW, 2 * rhs), F32),
        pltpu.VMEM((2, total * LOW, 2 * rhs), F32),
        pltpu.VMEM((4, rows, rhs, 2 * rhs), F32),
        pltpu.VMEM((4, cols, rhs, 2 * rhs), F32),
    ]
    held = sum(math.prod(b.shape) * jnp.dtype(b.dtype).itemsize for b in buffers)
    grant = min(held + (24 << 20), 62 << 20)
    return pl.pallas_call(
        functools.partial(kernel, rows, cols),
        out_shape=(out, out),
        in_specs=[vmem, in_hbm, in_hbm, pl.BlockSpec(memory_space=pltpu.SMEM), in_hbm, vmem],
        out_specs=(vmem, vmem),
        scratch_shapes=buffers + [
            dma((spans,)), dma, dma, dma((4,)), dma, dma,
            dma((2,)), dma((2,)), dma((2,)), dma((2,)),
            dma((2,)), dma((2,)), dma((4,)), dma((4,)), dma((4,)), dma((4,)),
        ],
        compiler_params=pltpu.CompilerParams(
            collective_id=0, has_side_effects=True, vmem_limit_bytes=grant
        ),
    )(right_sides, diag_tiles, factor, tile_ranks, inv_factor, sub_sizes.reshape(1, -1))


def solution(mesh):
    rows, cols = mesh.shape["row"], mesh.shape["col"]
    placed = (
        P(None, ("row", "col")),
        P(("row", "col"), None, None),
        P("row", "col", None, None, None, None),
        P("row", "col", None),
        P(("row", "col"), None, None, None),
        P(),
    )
    return jax.shard_map(
        functools.partial(body, rows, cols),
        mesh=mesh,
        in_specs=placed,
        out_specs=(P(None, ("row", "col")), P(None, ("row", "col"))),
        check_vma=False,
    )
```
